32 devices in a mesh: parts: 2 (over y), tmpl: 4 (over z), sta: 2 (over x), sub: 2 (over core).
Axes of the slice: x: 2, y: 2, z: 4, core: 2. Of those that a mesh axis runs over, the one named last changes fastest.
Arguments:
- traces: bfloat16 [16, 3, 1536], P(('tmpl', 'sta'), None, ('parts', 'sub')), parts along dimension 2
- trace_tail: bfloat16 [16, 3, 726], P(('tmpl', 'sta'), None, 'parts'), parts along dimension 2
- templates: bfloat16 [32, 3, 300], P('tmpl')
- win_lengths: int32 [32], replicated, may hold values from 150 to 300
- moveouts: int32 [32, 16], replicated, may hold values from 0 to 63
- chan_mask: int32 [32, 3], P('parts'), parts along dimension 0, may hold values 0 or 1
- subnet: int32 [16], replicated, may hold values from 0 to 1
Outputs:
- network_stack: float32 [32, 2, 1536], P(('tmpl', 'sta'), None, ('parts', 'sub')), parts along dimension 2
The draws below stay inside these ranges and needn't reach their ends.
There are 2 independent parts, one for each index of `parts`. The reference program is written for one: setup_inputs(seed, part) draws one part's arguments, and reference() takes and returns one part's arrays. A program takes and returns all parts, laid end to end along the dimension named above; an argument that names none is the same for every part. Nothing has to cross between parts.
All inputs are finite; a program needn't handle non-finite values.
Results may differ from the reference program's by a relative error of at most 0.0003.
Values may be sent and summed in bfloat16 or wider, within the bound.
No kernel may reach another device: no remote copies, remote signals or barrier semaphores. Data moves between devices by JAX's collectives and lax.ppermute only.
A program may use at most 64 MiB of HBM per device.

```python
import math
import jax
import jax.numpy as jnp
from jax import lax

TLEN = 300
MOVE = 64
REGIONS = 2
K_DEV = 8
HALO = 363
STATIONS = 16
TEMPLATES = 32
NT = 768


def rough_wave(key, dims_out, lowest, highest, block_len):
    noise_key, scale_key, env_key = jax.random.split(key, 3)
    noise_part = jnp.clip(jax.random.normal(noise_key, dims_out, jnp.float32), -6.0, 6.0)
    upper = highest
    scales = jnp.exp(jax.random.uniform(scale_key, dims_out[:2] + (1,), jnp.float32, math.log(lowest), math.log(upper)))
    block_count = -(-dims_out[2] // block_len)
    envelope = jnp.exp(jax.random.uniform(env_key, dims_out[:2] + (block_count,), jnp.float32, math.log(0.3), math.log(3.0)))
    envelope = jnp.repeat(envelope, block_len, axis=2)[:, :, :dims_out[2]]
    return (noise_part * scales * envelope).astype(jnp.bfloat16)


def draw_traces(key, part):
    return rough_wave(key, (STATIONS, 3, NT), 1.0, 10.0, 32)


def draw_trace_tail(key, part):
    return rough_wave(key, (STATIONS, 3, HALO), 1.0, 10.0, 32)


def draw_templates(key, part):
    return rough_wave(key, (TEMPLATES, 3, TLEN), 0.1, 1.0, 25)


def with_ends(result, key, smallest, high):
    index_at = [jax.random.randint(jax.random.fold_in(key, axis), (), 0, length) for axis, length in enumerate(result.shape)]
    main_axis = result.shape.index(max(result.shape))
    beside = index_at[:main_axis] + [(index_at[main_axis] + 1) % result.shape[main_axis]] + index_at[main_axis + 1:]
    return result.at[tuple(index_at)].set(smallest).at[tuple(beside)].set(high)


def setup_inputs(seed: int = 0, part: int = 0) -> dict:
    splits = jax.random.split(jax.random.key(seed), 8)
    part_keys = jax.random.split(jax.random.fold_in(splits[7], part), 8)
    traces = draw_traces(jax.random.fold_in(jax.random.fold_in(splits[7], part), 71), part)
    trace_tail = draw_trace_tail(jax.random.fold_in(jax.random.fold_in(splits[7], part), 71), part)
    templates = draw_templates(jax.random.fold_in(splits[7], 71), part)
    win_lengths = with_ends(jax.random.randint(splits[3], (TEMPLATES,), TLEN // 2, TLEN + 1), jax.random.fold_in(splits[3], 1), TLEN // 2, TLEN).astype(jnp.int32)
    moveouts = with_ends(jax.random.randint(splits[4], (TEMPLATES, STATIONS), 0, MOVE), jax.random.fold_in(splits[4], 1), 0, MOVE - 1).astype(jnp.int32)
    chan_mask = with_ends((jax.random.randint(part_keys[5], (STATIONS, 3), 0, 4) < 3).astype(jnp.int32), jax.random.fold_in(part_keys[5], 1), 0, 1)
    subnet = with_ends(jax.random.randint(splits[6], (STATIONS,), 0, REGIONS), jax.random.fold_in(splits[6], 1), 0, REGIONS - 1).astype(jnp.int32)
    return {"traces": traces, "trace_tail": trace_tail, "templates": templates, "win_lengths": win_lengths, "moveouts": moveouts, "chan_mask": chan_mask, "subnet": subnet}


def correlate(extended, tmpl_rows, win_rows, mask_rows, lag_rows, subnet_rows, t_out):
    span_len = tmpl_rows.shape[2]
    t_corr = extended.shape[2] - span_len + 1
    live_count = jnp.maximum(lax.optimization_barrier(jnp.sum(mask_rows, axis=1)), 1).astype(jnp.float32)
    weights = mask_rows.astype(jnp.float32)
    win_float = win_rows.astype(jnp.float32)
    running = jnp.zeros((extended.shape[0], tmpl_rows.shape[0], t_corr), jnp.float32)
    for channel in range(3):
        signal = extended[:, channel:channel + 1, :]
        corr = lax.conv_general_dilated(signal, tmpl_rows[:, channel:channel + 1, :], (1,), 'VALID', dimension_numbers=('NCH', 'OIH', 'NCH'), preferred_element_type=jnp.float32)
        squares = jnp.square(extended[:, channel, :].astype(jnp.float32))
        prefix = jnp.concatenate([jnp.zeros((squares.shape[0], 1), jnp.float32), jnp.cumsum(squares, axis=1)], axis=1)

        def window_sum(width):
            return lax.dynamic_slice_in_dim(prefix, width, t_corr, 1) - prefix[:, :t_corr]
        energy = jax.vmap(window_sum, out_axes=1)(win_rows.astype(jnp.int32))
        tmpl_norm = jnp.sqrt(lax.optimization_barrier(jnp.sum(jnp.square(tmpl_rows[:, channel, :].astype(jnp.float32)), axis=1)) + 1e-06)
        denom = tmpl_norm[None, :, None] * jnp.sqrt(energy + 1e-05 * win_float[None, :, None])
        running = running + weights[:, channel][:, None, None] * corr / denom
    coherent = running / live_count[:, None, None]

    def align(series_rows, shift_rows):
        return jax.vmap(lambda series, lag_value: lax.dynamic_slice_in_dim(series, lag_value, t_out, 0))(series_rows, shift_rows)
    aligned = jax.vmap(align)(coherent, jnp.transpose(lag_rows).astype(jnp.int32))
    member = (subnet_rows[:, None] == jnp.arange(REGIONS)[None, :]).astype(jnp.float32)
    return jnp.einsum('skt,sr->krt', aligned, member, precision=lax.Precision.HIGHEST)

def reference(traces, trace_tail, templates, win_lengths, moveouts, chan_mask, subnet):
    extended = jnp.concatenate([traces, trace_tail], axis=2)
    t_total = traces.shape[2]
    n_blocks = TEMPLATES // K_DEV
    tmpl_blocks = templates.reshape(n_blocks, K_DEV, 3, TLEN)
    win_blocks = win_lengths.reshape(n_blocks, K_DEV)
    lag_blocks = moveouts.reshape(n_blocks, K_DEV, STATIONS)

    def one_block(packed):
        return correlate(extended, packed[0], packed[1], chan_mask, packed[2], subnet, t_total)
    stacked = lax.map(one_block, (tmpl_blocks, win_blocks, lag_blocks))
    return stacked.reshape(TEMPLATES, REGIONS, t_total)
```

```python
import functools

import jax
import jax.numpy as jnp
from jax import lax
from jax.experimental import pallas as pl
from jax.experimental.pallas import tpu as pltpu
from jax.sharding import PartitionSpec as P

REGIONS = 2
CHANNELS = 3
LANES = 128


def ceil_to(value, unit):
    return -(-value // unit) * unit


def swap(block, axis, bit):
    size = lax.axis_size(axis)
    return lax.ppermute(block, axis, [(i, i ^ bit) for i in range(size)])


def halo_rows(traces, trace_tail, width):
    st_dev, channels, t_dev = traces.shape
    rim_len = trace_tail.shape[2]
    rows = ceil_to(channels * st_dev, 8)
    size = lax.axis_size("sub")
    rim = lax.ppermute(traces, "sub", [(i + 1, i) for i in range(size - 1)])
    last = lax.axis_index("sub") == size - 1
    rim = jnp.where(last, trace_tail, rim[:, :, :rim_len])
    extended = jnp.concatenate([traces, rim], axis=2)
    extended = jnp.transpose(extended, (1, 0, 2)).reshape(channels * st_dev, t_dev + rim_len)
    return jnp.pad(extended, ((0, rows - channels * st_dev), (0, width - t_dev - rim_len)))


def column(row, size):
    square = jnp.broadcast_to(row, (size, size))
    diagonal = lax.broadcasted_iota(jnp.int32, (size, size), 0) == lax.broadcasted_iota(
        jnp.int32, (size, size), 1
    )
    return jnp.sum(jnp.where(diagonal, square, jnp.zeros_like(square)), axis=1, keepdims=True)


def stack_kernel(
    masks, st_dev, t_corr, t_out, share,
    win_ref, signal_ref, tmpl_ref, lag_ref, mask_ref, subnet_ref, out_ref, tmpl_rows,
):
    stations = mask_ref.shape[0]
    slot_rows, width = signal_ref.shape
    slots = 1 << len(masks)
    rows = slot_rows // slots
    tmpl_dev, span = tmpl_ref.shape[1:]
    blocks = -(-t_corr // LANES)
    depth = ceil_to(LANES - 1 + span, LANES)
    reach = LANES * (blocks - 1) + depth
    sta_index = lax.axis_index("sta")
    tmpl_index = lax.axis_index("tmpl")
    me = tmpl_index * lax.axis_size("sta") + sta_index
    first = sta_index * share
    f32, bf16 = jnp.float32, jnp.bfloat16

    col = lax.broadcasted_iota(jnp.int32, (stations, slot_rows), 1)
    row = lax.broadcasted_iota(jnp.int32, (stations, slot_rows), 0)
    slot, inner = col // rows, col % rows
    group = jnp.full((stations, slot_rows), me, jnp.int32)
    for bit, mask in enumerate(masks):
        group = group ^ (((slot >> bit) & 1) * mask)
    station = jnp.where(inner < CHANNELS * st_dev, group * st_dev + inner % st_dev, -1)
    signal = signal_ref[...]

    for channel in range(CHANNELS):
        padded = jnp.zeros((tmpl_dev, depth), f32)
        tmpl_rows[channel, :, :] = padded
        tmpl_rows[channel, :, :span] = tmpl_ref[channel].astype(f32)

    lag_q = lax.broadcasted_iota(jnp.int32, (LANES, depth), 1) - lax.broadcasted_iota(
        jnp.int32, (LANES, depth), 0
    )
    bands, floors = [], []
    for k in range(share):
        win = win_ref[tmpl_index * tmpl_dev + first + k]
        inside = (lag_q >= 0) & (lag_q < win)
        bands.append(jnp.where(inside, 2.0, 0.0).astype(bf16))
        floors.append(jnp.full((1, LANES), win.astype(f32) * 1e-05, f32))
    band = jnp.concatenate(bands, axis=0)
    floor = jnp.concatenate(floors, axis=1)

    mask = mask_ref[...].astype(f32)
    live = jnp.maximum(jnp.sum(mask, axis=1, keepdims=True), 1.0)
    contract = (((1,), (1,)), ((), ()))

    def windows(value):
        return jnp.concatenate(
            [value[:, LANES * a : LANES * a + depth] for a in range(blocks)], axis=0
        )

    coherent = jnp.zeros((blocks * stations, share * LANES), f32)
    for channel in range(CHANNELS):
        select = (station == row) & (inner // st_dev == channel)
        wave = jnp.dot(
            jnp.where(select, 1.0, 0.0).astype(bf16), signal, preferred_element_type=f32
        )
        wave = jnp.concatenate([wave, jnp.zeros((stations, reach - width), f32)], axis=1)
        half = 0.5 * wave * wave
        upper = half.astype(bf16)
        lower = (half - upper.astype(f32)).astype(bf16)
        energy = lax.dot_general(
            jnp.concatenate([windows(upper), windows(lower)], axis=0), band, contract,
            preferred_element_type=f32,
        )
        energy = energy[: blocks * stations] + energy[blocks * stations :]
        toeplitz, norms = [], []
        for k in range(share):
            taps = tmpl_rows[channel, pl.ds(first + k, 1), :]
            power = jnp.sum(taps * taps, axis=1, keepdims=True)
            norms.append(jnp.broadcast_to(jnp.sqrt(power + 1e-06), (1, LANES)))
            spread = jnp.broadcast_to(taps, (LANES, depth))
            toeplitz.append(
                pltpu.roll(spread, 0, 1, stride=1, stride_axis=0).astype(bf16)
            )
        corr = lax.dot_general(
            windows(wave.astype(bf16)), jnp.concatenate(toeplitz, axis=0), contract,
            preferred_element_type=f32,
        )
        denom = jnp.concatenate(norms, axis=1) * jnp.sqrt(energy + floor)
        weight = jnp.concatenate([mask[:, channel : channel + 1]] * blocks, axis=0)
        coherent = coherent + weight * corr / denom
    coherent = coherent / jnp.concatenate([live] * blocks, axis=0)

    member = column(subnet_ref[...], stations)
    for k in range(share):
        series = jnp.concatenate(
            [
                coherent[a * stations : (a + 1) * stations, k * LANES : (k + 1) * LANES]
                for a in range(blocks)
            ],
            axis=1,
        )
        lag = column(lag_ref[pl.ds(tmpl_index * tmpl_dev + first + k, 1), :], stations)
        step = 1
        while step <= t_corr - t_out:
            moved = pltpu.roll(series, blocks * LANES - step, 1)
            series = jnp.where((lag & step) != 0, moved, series)
            step *= 2
        aligned = series[:, :t_out]
        for region in range(REGIONS):
            picked = jnp.where(member == region, aligned, 0.0)
            out_ref[k, region : region + 1, :] = jnp.sum(picked, axis=0, keepdims=True)


def shards(traces, trace_tail, templates, win_lengths, moveouts, chan_mask, subnet):
    st_dev, channels, t_dev = traces.shape
    rim_len = trace_tail.shape[2]
    tmpl_dev, _, span = templates.shape
    t_corr = t_dev + rim_len - span + 1
    tmpl_count, sta_count = lax.axis_size("tmpl"), lax.axis_size("sta")
    share = tmpl_dev // sta_count
    gathered = halo_rows(traces, trace_tail, ceil_to(t_dev + rim_len, LANES))
    masks = []
    for axis, scale in (("tmpl", sta_count), ("sta", 1)):
        bit = lax.axis_size(axis) // 2
        while bit:
            gathered = jnp.concatenate([gathered, swap(gathered, axis, bit)], axis=0)
            masks.append(bit * scale)
            bit //= 2
    vmem = pl.BlockSpec(memory_space=pltpu.VMEM)
    kernel = functools.partial(stack_kernel, tuple(masks), st_dev, t_corr, t_dev, share)
    return pl.pallas_call(
        kernel,
        out_shape=jax.ShapeDtypeStruct((share, REGIONS, t_dev), jnp.float32),
        in_specs=[pl.BlockSpec(memory_space=pltpu.SMEM)] + [vmem] * 5,
        out_specs=vmem,
        scratch_shapes=[
            pltpu.VMEM((channels, tmpl_dev, ceil_to(LANES - 1 + span, LANES)), jnp.float32)
        ],
    )(
        win_lengths, gathered, jnp.transpose(templates, (1, 0, 2)), moveouts, chan_mask,
        subnet.reshape(1, -1),
    )


def solution(mesh):
    in_specs = (
        P(("tmpl", "sta"), None, ("parts", "sub")),
        P(("tmpl", "sta"), None, "parts"),
        P("tmpl", None, None),
        P(),
        P(),
        P("parts", None),
        P(),
    )
    out_specs = P(("tmpl", "sta"), None, ("parts", "sub"))
    return jax.shard_map(shards, mesh=mesh, in_specs=in_specs, out_specs=out_specs, check_vma=False)
```

```python
import functools

import jax
import jax.numpy as jnp
from jax import lax
from jax.experimental import pallas as pl
from jax.experimental.pallas import tpu as pltpu
from jax.sharding import PartitionSpec as P

REGIONS = 2
CHANNELS = 3
LANES = 128
BLOCK = 64


def ceil_to(value, unit):
    return -(-value // unit) * unit


def swap(block, axis, bit):
    size = lax.axis_size(axis)
    return lax.ppermute(block, axis, [(i, i ^ bit) for i in range(size)])


def halo_rows(traces, trace_tail, width):
    t_dev, rim_len = traces.shape[2], trace_tail.shape[2]
    size = lax.axis_size("sub")
    rim = lax.ppermute(traces, "sub", [(i, (i - 1) % size) for i in range(size)])
    last = lax.axis_index("sub") == size - 1
    rim = jnp.where(last, trace_tail, rim[:, :, :rim_len])
    extended = jnp.transpose(jnp.concatenate([traces, rim], axis=2), (1, 0, 2))
    return jnp.pad(extended, ((0, 0), (0, 0), (0, width - t_dev - rim_len)))


def prep_kernel(
    masks, st_dev, share, win_ref, tmpl_ref, lag_ref, mask_ref, subnet_ref,
    toeplitz_ref, band_ref, rows_ref, weight_ref, shift_ref, member_ref, taps_ref,
):
    f32, bf16 = jnp.float32, jnp.bfloat16
    stations = mask_ref.shape[1]
    tmpl_dev, span = tmpl_ref.shape[1:]
    depth = band_ref.shape[1]
    padded = band_ref.shape[0] // BLOCK
    sta_index = lax.axis_index("sta")
    tmpl_index = lax.axis_index("tmpl")
    me = tmpl_index * lax.axis_size("sta") + sta_index
    first = sta_index * share

    taps_ref[...] = jnp.zeros(taps_ref.shape, f32)
    taps_ref[:, :, :span] = tmpl_ref[...].astype(f32)
    lag_q = lax.broadcasted_iota(jnp.int32, (BLOCK, depth), 1) - lax.broadcasted_iota(
        jnp.int32, (BLOCK, depth), 0
    )
    for k in range(padded):
        at = first + min(k, share - 1)
        span_rows = slice(k * BLOCK, (k + 1) * BLOCK)
        win = win_ref[tmpl_index * tmpl_dev + at]
        inside = (lag_q >= 0) & (lag_q < win)
        band_ref[span_rows, :] = jnp.where(inside, 2.0, 0.0).astype(bf16)
        rows_ref[CHANNELS : CHANNELS + 1, span_rows] = jnp.full(
            (1, BLOCK), win.astype(f32) * 1e-05, f32
        )
        for channel in range(CHANNELS):
            taps = taps_ref[channel, pl.ds(at, 1), :]
            power = jnp.sum(taps * taps, axis=1, keepdims=True)
            rows_ref[channel : channel + 1, span_rows] = jnp.broadcast_to(
                jnp.sqrt(power + 1e-06), (1, BLOCK)
            )
            toeplitz_ref[channel, span_rows, :] = pltpu.roll(
                jnp.broadcast_to(taps, (BLOCK, depth)), 0, 1, stride=1, stride_axis=0
            ).astype(bf16)

    row = lax.broadcasted_iota(jnp.int32, (stations, stations), 0)
    lane = lax.broadcasted_iota(jnp.int32, (stations, stations), 1)
    slot = row // st_dev
    group = jnp.full((stations, stations), me, jnp.int32)
    for bit, mask in enumerate(masks):
        group = group ^ (((slot >> bit) & 1) * mask)
    chosen = lane == group * st_dev + row % st_dev

    def column(value):
        value = jnp.broadcast_to(value, (stations, stations))
        value = jnp.sum(jnp.where(chosen, value, 0.0), axis=1, keepdims=True)
        return jnp.broadcast_to(value, (stations, LANES))

    mask = mask_ref[...].astype(f32)
    live = jnp.maximum(jnp.sum(mask, axis=0, keepdims=True), 1.0)
    for channel in range(CHANNELS):
        weight_ref[channel] = column(mask[channel : channel + 1, :] / live)
    member_ref[...] = column(subnet_ref[...].astype(f32))
    lags = jnp.dot(
        jnp.where(chosen, 1.0, 0.0).astype(bf16), lag_ref[...].astype(f32).astype(bf16),
        preferred_element_type=f32,
    )
    wide = lax.broadcasted_iota(jnp.int32, lags.shape, 1)
    for k in range(share):
        own = jnp.where(wide == tmpl_index * tmpl_dev + first + k, lags, 0.0)
        own = jnp.sum(own, axis=1, keepdims=True).astype(jnp.int32)
        shift_ref[k] = jnp.broadcast_to(own, (stations, LANES))


def stack_kernel(
    start, t_corr, t_out, share, signal_ref, toeplitz_ref, band_ref, rows_ref, weight_ref,
    shift_ref, member_ref, *partial_and_out,
):
    f32, bf16 = jnp.float32, jnp.bfloat16
    out_ref = partial_and_out[-1]
    count, width = signal_ref.shape[1:]
    columns, depth = band_ref.shape
    blocks = -(-t_corr // BLOCK)
    pairs = -(-blocks // 2)
    own = slice(start, start + count)
    contract = (((1,), (1,)), ((), ()))

    def windows(value):
        odd = pltpu.roll(value, width - BLOCK, 1)
        pieces = []
        for a in range(blocks):
            base = LANES * (a // 2)
            pieces.append((odd if a % 2 else value)[:, base : base + depth])
        return jnp.concatenate(pieces, axis=0)

    waves, squares = [], []
    for channel in range(CHANNELS):
        wave = signal_ref[channel].astype(f32)
        half = 0.5 * wave * wave
        upper = half.astype(bf16).astype(f32)
        waves.append(windows(wave).astype(bf16))
        squares += [windows(upper), windows(half - upper)]
    energies = lax.dot_general(
        jnp.concatenate(squares, axis=0).astype(bf16), band_ref[...], contract,
        preferred_element_type=f32,
    ).reshape(2 * CHANNELS, blocks, count, columns)
    coherent = jnp.zeros((blocks, count, columns), f32)
    floor = rows_ref[CHANNELS : CHANNELS + 1, :]
    for channel in range(CHANNELS):
        corr = lax.dot_general(
            waves[channel], toeplitz_ref[channel], contract, preferred_element_type=f32
        ).reshape(blocks, count, columns)
        energy = energies[2 * channel] + energies[2 * channel + 1]
        denom = rows_ref[channel : channel + 1, :] * jnp.sqrt(energy + floor)
        weight = jnp.concatenate([weight_ref[channel, own, :]] * (columns // LANES), axis=1)
        coherent = coherent + weight * corr / denom

    low = lax.broadcasted_iota(jnp.int32, (count, LANES), 1) < BLOCK
    member = member_ref[own, :]
    member = jnp.concatenate([member] * -(-t_out // LANES), axis=1)[:, :t_out]
    for k in range(share):
        base = LANES * (k // 2)
        pieces = []
        for pair in range(pairs):
            even = coherent[2 * pair, :, base : base + LANES]
            odd = coherent[min(2 * pair + 1, blocks - 1), :, base : base + LANES]
            if k % 2:
                even = pltpu.roll(even, BLOCK, 1)
            else:
                odd = pltpu.roll(odd, BLOCK, 1)
            pieces.append(jnp.where(low, even, odd))
        series = jnp.concatenate(pieces, axis=1)
        lag = jnp.concatenate([shift_ref[k, own, :]] * pairs, axis=1)
        step = 1
        while step <= t_corr - t_out:
            moved = pltpu.roll(series, pairs * LANES - step, 1)
            series = jnp.where((lag & step) != 0, moved, series)
            step *= 2
        aligned = series[:, :t_out]
        for region in range(REGIONS):
            total = jnp.sum(jnp.where(member == region, aligned, 0.0), axis=0, keepdims=True)
            if len(partial_and_out) > 1:
                total = total + partial_and_out[0][k, region : region + 1, :]
            out_ref[k, region : region + 1, :] = total


def shards(traces, trace_tail, templates, win_lengths, moveouts, chan_mask, subnet):
    st_dev, channels, t_dev = traces.shape
    stations = chan_mask.shape[0]
    tmpl_dev, _, span = templates.shape
    t_corr = t_dev + trace_tail.shape[2] - span + 1
    tmpl_count, sta_count = lax.axis_size("tmpl"), lax.axis_size("sta")
    share = tmpl_dev // sta_count
    depth = ceil_to(BLOCK - 1 + span, LANES)
    columns = ceil_to(share * BLOCK, LANES)
    width = LANES * ((-(-t_corr // BLOCK) - 1) // 2) + depth
    width = max(width, ceil_to(t_dev + trace_tail.shape[2], LANES))
    vmem = pl.BlockSpec(memory_space=pltpu.VMEM)
    near = lambda value: pltpu.with_memory_space_constraint(value, pltpu.VMEM)

    rounds = []
    for axis, scale in (("tmpl", sta_count), ("sta", 1)):
        bit = lax.axis_size(axis) // 2
        while bit:
            rounds.append((axis, bit, bit * scale))
            bit //= 2
    masks = tuple(mask for _, _, mask in rounds)
    prepared = pl.pallas_call(
        functools.partial(prep_kernel, masks, st_dev, share),
        out_shape=(
            pltpu.VMEM((channels, columns, depth), jnp.bfloat16),
            pltpu.VMEM((columns, depth), jnp.bfloat16),
            pltpu.VMEM((8, columns), jnp.float32),
            pltpu.VMEM((channels, stations, LANES), jnp.float32),
            pltpu.VMEM((share, stations, LANES), jnp.int32),
            pltpu.VMEM((stations, LANES), jnp.float32),
        ),
        in_specs=[pl.BlockSpec(memory_space=pltpu.SMEM)] + [vmem] * 4,
        out_specs=(vmem,) * 6,
        scratch_shapes=[pltpu.VMEM((channels, tmpl_dev, depth), jnp.float32)],
        name="prep",
    )(
        win_lengths, jnp.transpose(templates, (1, 0, 2)), jnp.transpose(moveouts),
        jnp.transpose(chan_mask), subnet.reshape(1, -1),
    )
    prepared = tuple(near(value) for value in prepared)

    def stack(start, signal, *partial):
        shape = (share, REGIONS, t_dev)
        operands = (near(signal),) + prepared + partial
        return pl.pallas_call(
            functools.partial(stack_kernel, start, t_corr, t_dev, share),
            out_shape=jax.ShapeDtypeStruct(shape, jnp.float32)
            if partial
            else pltpu.VMEM(shape, jnp.float32),
            in_specs=[vmem] * len(operands),
            out_specs=vmem,
            name="late" if partial else "early",
        )(*operands)

    gathered = halo_rows(traces, trace_tail, width)
    for axis, bit, _ in rounds[:-1]:
        gathered = jnp.concatenate([gathered, swap(gathered, axis, bit)], axis=1)
    arriving = swap(gathered, rounds[-1][0], rounds[-1][1])
    partial = stack(0, gathered)
    return stack(gathered.shape[1], arriving, near(partial))


def solution(mesh):
    in_specs = (
        P(("tmpl", "sta"), None, ("parts", "sub")),
        P(("tmpl", "sta"), None, "parts"),
        P("tmpl", None, None),
        P(),
        P(),
        P("parts", None),
        P(),
    )
    out_specs = P(("tmpl", "sta"), None, ("parts", "sub"))
    return jax.shard_map(shards, mesh=mesh, in_specs=in_specs, out_specs=out_specs, check_vma=False)
```

```python
import functools

import jax
import jax.numpy as jnp
from jax import lax
from jax.experimental import pallas as pl
from jax.experimental.pallas import tpu as pltpu
from jax.sharding import PartitionSpec as P

REGIONS = 2
CHANNELS = 3
LANES = 128
BLOCK = 64


def ceil_to(value, unit):
    return -(-value // unit) * unit


def cross(block, axis, bit):
    pairs = [(2 * i + c, 2 * (i ^ bit) + 1 - c) for i in range(lax.axis_size(axis)) for c in (0, 1)]
    return lax.ppermute(block, (axis, "sub"), pairs)


def whole_rows(traces, trace_tail, width):
    t_dev = traces.shape[2]
    other = lax.ppermute(traces, "sub", [(0, 1), (1, 0)])
    second = lax.axis_index("sub") == 1
    own = jnp.concatenate([traces, traces, trace_tail], axis=2)
    own = jnp.transpose(own, (1, 0, 2))
    own = jnp.pad(own, ((0, 0), (0, 0), (0, width - own.shape[2])))
    own = lax.optimization_barrier(own)
    other = jnp.transpose(other, (1, 0, 2))
    left = jnp.where(second, other, own[:, :, :t_dev])
    right = jnp.where(second, own[:, :, t_dev : 2 * t_dev], other)
    return jnp.concatenate([left, right, own[:, :, 2 * t_dev :]], axis=2)


def prep_kernel(
    masks, st_dev, share, win_ref, tmpl_ref, lag_ref, mask_ref, subnet_ref,
    toeplitz_ref, band_ref, rows_ref, weight_ref, shift_ref, member_ref, taps_ref,
):
    f32, bf16 = jnp.float32, jnp.bfloat16
    stations = mask_ref.shape[1]
    tmpl_dev, span = tmpl_ref.shape[1:]
    depth = band_ref.shape[1]
    padded = band_ref.shape[0] // BLOCK
    sta_index = lax.axis_index("sta")
    tmpl_index = lax.axis_index("tmpl")
    me = tmpl_index * lax.axis_size("sta") + sta_index
    first = sta_index * share

    taps_ref[...] = jnp.zeros(taps_ref.shape, f32)
    taps_ref[:, :, :span] = tmpl_ref[...].astype(f32)
    lag_q = lax.broadcasted_iota(jnp.int32, (BLOCK, depth), 1) - lax.broadcasted_iota(
        jnp.int32, (BLOCK, depth), 0
    )
    for k in range(padded):
        at = first + min(k, share - 1)
        span_rows = slice(k * BLOCK, (k + 1) * BLOCK)
        win = win_ref[tmpl_index * tmpl_dev + at]
        inside = (lag_q >= 0) & (lag_q < win)
        band_ref[span_rows, :] = jnp.where(inside, 2.0, 0.0).astype(bf16)
        rows_ref[CHANNELS : CHANNELS + 1, span_rows] = jnp.full(
            (1, BLOCK), win.astype(f32) * 1e-05, f32
        )
        for channel in range(CHANNELS):
            taps = taps_ref[channel, pl.ds(at, 1), :]
            power = jnp.sum(taps * taps, axis=1, keepdims=True)
            rows_ref[channel : channel + 1, span_rows] = jnp.broadcast_to(
                jnp.sqrt(power + 1e-06), (1, BLOCK)
            )
            toeplitz_ref[channel, span_rows, :] = pltpu.roll(
                jnp.broadcast_to(taps, (BLOCK, depth)), 0, 1, stride=1, stride_axis=0
            ).astype(bf16)

    row = lax.broadcasted_iota(jnp.int32, (stations, stations), 0)
    lane = lax.broadcasted_iota(jnp.int32, (stations, stations), 1)
    slot = row // st_dev
    group = jnp.full((stations, stations), me, jnp.int32)
    for bit, mask in enumerate(masks):
        group = group ^ (((slot >> bit) & 1) * mask)
    chosen = lane == group * st_dev + row % st_dev

    def column(value):
        value = jnp.broadcast_to(value, (stations, stations))
        value = jnp.sum(jnp.where(chosen, value, 0.0), axis=1, keepdims=True)
        return jnp.broadcast_to(value, (stations, LANES))

    mask = mask_ref[...].astype(f32)
    live = jnp.maximum(jnp.sum(mask, axis=0, keepdims=True), 1.0)
    for channel in range(CHANNELS):
        weight_ref[channel] = column(mask[channel : channel + 1, :] / live)
    member_ref[...] = column(subnet_ref[...].astype(f32))
    lags = jnp.dot(
        jnp.where(chosen, 1.0, 0.0).astype(bf16), lag_ref[...].astype(f32).astype(bf16),
        preferred_element_type=f32,
    )
    wide = lax.broadcasted_iota(jnp.int32, lags.shape, 1)
    for k in range(share):
        own = jnp.where(wide == tmpl_index * tmpl_dev + first + k, lags, 0.0)
        own = jnp.sum(own, axis=1, keepdims=True).astype(jnp.int32)
        shift_ref[k] = own + lax.broadcasted_iota(jnp.int32, (stations, LANES), 1)


def stack_kernel(
    start, t_corr, t_out, share, signal_ref, toeplitz_ref, band_ref, rows_ref, weight_ref,
    shift_ref, member_ref, *partial_and_out,
):
    f32, bf16 = jnp.float32, jnp.bfloat16
    out_ref = partial_and_out[-1]
    count = signal_ref.shape[1]
    columns, depth = band_ref.shape
    blocks = -(-t_corr // BLOCK)
    width = LANES * ((blocks - 1) // 2) + depth
    if signal_ref.shape[2] > width:
        begin = pl.multiple_of(lax.axis_index("sub") * t_out, LANES)
    else:
        begin = 0
    own = slice(start, start + count)
    contract = (((1,), (1,)), ((), ()))

    def windows(value):
        odd = pltpu.roll(value, width - BLOCK, 1)
        pieces = []
        for a in range(blocks):
            base = LANES * (a // 2)
            pieces.append((odd if a % 2 else value)[:, base : base + depth])
        return jnp.concatenate(pieces, axis=0)

    waves, squares = [], []
    for channel in range(CHANNELS):
        wave = signal_ref[channel, :, pl.ds(begin, width)].astype(f32)
        half = 0.5 * wave * wave
        upper = half.astype(bf16).astype(f32)
        waves.append(windows(wave).astype(bf16))
        squares += [windows(upper), windows(half - upper)]
    energies = lax.dot_general(
        jnp.concatenate(squares, axis=0).astype(bf16), band_ref[...], contract,
        preferred_element_type=f32,
    ).reshape(2 * CHANNELS, blocks, count, columns)
    coherent = jnp.zeros((blocks, count, columns), f32)
    floor = rows_ref[CHANNELS : CHANNELS + 1, :]
    for channel in range(CHANNELS):
        corr = lax.dot_general(
            waves[channel], toeplitz_ref[channel], contract, preferred_element_type=f32
        ).reshape(blocks, count, columns)
        energy = energies[2 * channel] + energies[2 * channel + 1]
        denom = rows_ref[channel : channel + 1, :] * jnp.sqrt(energy + floor)
        weight = jnp.concatenate([weight_ref[channel, own, :]] * (columns // LANES), axis=1)
        coherent = coherent + weight * corr / denom

    tiles = t_out // LANES
    member = jnp.concatenate([member_ref[own, :]] * tiles, axis=1)
    for k in range(share):
        base = LANES * (k // 2)
        target = shift_ref[k, own, :]
        lane = target % BLOCK + BLOCK * (k % 2)
        moved = [
            jnp.take_along_axis(
                coherent[a, :, base : base + LANES], lane, axis=1, mode="promise_in_bounds"
            )
            for a in range(blocks)
        ]
        aligned = jnp.concatenate(
            [
                jnp.where(
                    target < BLOCK,
                    moved[2 * tile],
                    jnp.where(target < LANES, moved[2 * tile + 1], moved[2 * tile + 2]),
                )
                for tile in range(tiles)
            ],
            axis=1,
        )
        for region in range(REGIONS):
            total = jnp.sum(jnp.where(member == region, aligned, 0.0), axis=0, keepdims=True)
            if len(partial_and_out) > 1:
                total = total + partial_and_out[0][k, region : region + 1, :]
            out_ref[k, region : region + 1, :] = total


def shards(traces, trace_tail, templates, win_lengths, moveouts, chan_mask, subnet):
    st_dev, channels, t_dev = traces.shape
    stations = chan_mask.shape[0]
    tmpl_dev, _, span = templates.shape
    t_corr = t_dev + trace_tail.shape[2] - span + 1
    tmpl_count, sta_count = lax.axis_size("tmpl"), lax.axis_size("sta")
    share = tmpl_dev // sta_count
    depth = ceil_to(BLOCK - 1 + span, LANES)
    columns = ceil_to(share * BLOCK, LANES)
    width = LANES * ((-(-t_corr // BLOCK) - 1) // 2) + depth
    vmem = pl.BlockSpec(memory_space=pltpu.VMEM)
    near = lambda value: pltpu.with_memory_space_constraint(value, pltpu.VMEM)

    rounds = []
    for axis, scale in (("tmpl", sta_count), ("sta", 1)):
        bit = lax.axis_size(axis) // 2
        while bit:
            rounds.append((axis, bit, bit * scale))
            bit //= 2
    masks = tuple(mask for _, _, mask in rounds)
    prepared = pl.pallas_call(
        functools.partial(prep_kernel, masks, st_dev, share),
        out_shape=(
            pltpu.VMEM((channels, columns, depth), jnp.bfloat16),
            pltpu.VMEM((columns, depth), jnp.bfloat16),
            pltpu.VMEM((8, columns), jnp.float32),
            pltpu.VMEM((channels, stations, LANES), jnp.float32),
            pltpu.VMEM((share, stations, LANES), jnp.int32),
            pltpu.VMEM((stations, LANES), jnp.float32),
        ),
        in_specs=[pl.BlockSpec(memory_space=pltpu.SMEM)] + [vmem] * 4,
        out_specs=(vmem,) * 6,
        scratch_shapes=[pltpu.VMEM((channels, tmpl_dev, depth), jnp.float32)],
        name="prep",
    )(
        win_lengths, jnp.transpose(templates, (1, 0, 2)), jnp.transpose(moveouts),
        jnp.transpose(chan_mask), subnet.reshape(1, -1),
    )
    prepared = tuple(near(value) for value in prepared)

    def stack(start, signal, *partial):
        shape = (share, REGIONS, t_dev)
        operands = (near(signal),) + prepared + partial
        return pl.pallas_call(
            functools.partial(stack_kernel, start, t_corr, t_dev, share),
            out_shape=jax.ShapeDtypeStruct(shape, jnp.float32)
            if partial
            else pltpu.VMEM(shape, jnp.float32),
            in_specs=[vmem] * len(operands),
            out_specs=vmem,
            name="late" if partial else "early",
        )(*operands)

    gathered = whole_rows(traces, trace_tail, t_dev + width)
    for axis, bit, _ in rounds[:-1]:
        gathered = jnp.concatenate([gathered, cross(gathered, axis, bit)], axis=1)
    gathered, member = lax.optimization_barrier((gathered, prepared[-1]))
    prepared = prepared[:-1] + (near(member),)
    wanted = jnp.where(
        lax.axis_index("sub") == 1, gathered[:, :, :width], gathered[:, :, t_dev : t_dev + width]
    )
    arriving = cross(wanted, rounds[-1][0], rounds[-1][1])
    partial = stack(0, gathered)
    return stack(gathered.shape[1], arriving, near(partial))


def solution(mesh):
    in_specs = (
        P(("tmpl", "sta"), None, ("parts", "sub")),
        P(("tmpl", "sta"), None, "parts"),
        P("tmpl", None, None),
        P(),
        P(),
        P("parts", None),
        P(),
    )
    out_specs = P(("tmpl", "sta"), None, ("parts", "sub"))
    return jax.shard_map(shards, mesh=mesh, in_specs=in_specs, out_specs=out_specs, check_vma=False)
```

```python
import functools

import jax
import jax.numpy as jnp
from jax import lax
from jax.experimental import pallas as pl
from jax.experimental.pallas import tpu as pltpu
from jax.sharding import PartitionSpec as P

REGIONS = 2
CHANNELS = 3
LANES = 128
BLOCK = 64


def ceil_to(value, unit):
    return -(-value // unit) * unit


def cross(block, axis, bit):
    pairs = [(2 * i + c, 2 * (i ^ bit) + 1 - c) for i in range(lax.axis_size(axis)) for c in (0, 1)]
    return lax.ppermute(block, (axis, "sub"), pairs)


def whole_rows(traces, trace_tail, width):
    t_dev = traces.shape[2]
    other = lax.ppermute(traces, "sub", [(0, 1), (1, 0)])
    second = lax.axis_index("sub") == 1
    own = jnp.concatenate([traces, traces, trace_tail], axis=2)
    own = jnp.transpose(own, (1, 0, 2))
    own = jnp.pad(own, ((0, 0), (0, 0), (0, width - own.shape[2])))
    own = lax.optimization_barrier(own)
    other = jnp.transpose(other, (1, 0, 2))
    left = jnp.where(second, other, own[:, :, :t_dev])
    right = jnp.where(second, own[:, :, t_dev : 2 * t_dev], other)
    return jnp.concatenate([left, right, own[:, :, 2 * t_dev :]], axis=2)


def prep_kernel(
    masks, st_dev, share, win_ref, tmpl_ref, lag_ref, mask_ref, subnet_ref,
    toeplitz_ref, band_ref, rows_ref, weight_ref, shift_ref, member_ref, taps_ref,
):
    f32, bf16 = jnp.float32, jnp.bfloat16
    stations = mask_ref.shape[1]
    tmpl_dev, span = tmpl_ref.shape[1:]
    depth = band_ref.shape[1]
    padded = band_ref.shape[0] // BLOCK
    sta_index = lax.axis_index("sta")
    tmpl_index = lax.axis_index("tmpl")
    me = tmpl_index * lax.axis_size("sta") + sta_index
    first = sta_index * share

    taps_ref[...] = jnp.zeros(taps_ref.shape, f32)
    taps_ref[:, :, :span] = tmpl_ref[...].astype(f32)
    lag_q = lax.broadcasted_iota(jnp.int32, (BLOCK, depth), 1) - lax.broadcasted_iota(
        jnp.int32, (BLOCK, depth), 0
    )
    for k in range(padded):
        at = first + min(k, share - 1)
        span_rows = slice(k * BLOCK, (k + 1) * BLOCK)
        win = win_ref[tmpl_index * tmpl_dev + at]
        inside = (lag_q >= 0) & (lag_q < win)
        band_ref[span_rows, :] = jnp.where(inside, 2.0, 0.0).astype(bf16)
        rows_ref[CHANNELS : CHANNELS + 1, span_rows] = jnp.full(
            (1, BLOCK), win.astype(f32) * 1e-05, f32
        )
        for channel in range(CHANNELS):
            taps = taps_ref[channel, pl.ds(at, 1), :]
            power = jnp.sum(taps * taps, axis=1, keepdims=True)
            rows_ref[channel : channel + 1, span_rows] = jnp.broadcast_to(
                jnp.sqrt(power + 1e-06), (1, BLOCK)
            )
            toeplitz_ref[channel, span_rows, :] = pltpu.roll(
                jnp.broadcast_to(taps, (BLOCK, depth)), 0, 1, stride=1, stride_axis=0
            ).astype(bf16)

    row = lax.broadcasted_iota(jnp.int32, (stations, stations), 0)
    lane = lax.broadcasted_iota(jnp.int32, (stations, stations), 1)
    slot = row // st_dev
    group = jnp.full((stations, stations), me, jnp.int32)
    for bit, mask in enumerate(masks):
        group = group ^ (((slot >> bit) & 1) * mask)
    chosen = lane == group * st_dev + row % st_dev

    def column(value):
        value = jnp.broadcast_to(value, (stations, stations))
        value = jnp.sum(jnp.where(chosen, value, 0.0), axis=1, keepdims=True)
        return jnp.broadcast_to(value, (stations, LANES))

    mask = mask_ref[...].astype(f32)
    live = jnp.maximum(jnp.sum(mask, axis=0, keepdims=True), 1.0)
    for channel in range(CHANNELS):
        weight = column(mask[channel : channel + 1, :] / live)
        weight = jnp.concatenate([weight] * (weight_ref.shape[2] // LANES), axis=1)
        weight_ref[channel] = weight / rows_ref[channel : channel + 1, :]
    member_ref[...] = column(subnet_ref[...].astype(f32))
    lags = jnp.dot(
        jnp.where(chosen, 1.0, 0.0).astype(bf16), lag_ref[...].astype(f32).astype(bf16),
        preferred_element_type=f32,
    )
    wide = lax.broadcasted_iota(jnp.int32, lags.shape, 1)
    for k in range(share):
        own = jnp.where(wide == tmpl_index * tmpl_dev + first + k, lags, 0.0)
        own = jnp.sum(own, axis=1, keepdims=True).astype(jnp.int32)
        shift_ref[k] = own + lax.broadcasted_iota(jnp.int32, (stations, LANES), 1)


def stack_kernel(
    start, t_corr, t_out, share, signal_ref, toeplitz_ref, band_ref, rows_ref, weight_ref,
    shift_ref, member_ref, *partial_and_out,
):
    f32, bf16 = jnp.float32, jnp.bfloat16
    out_ref = partial_and_out[-1]
    count = signal_ref.shape[1]
    columns, depth = band_ref.shape
    blocks = -(-t_corr // BLOCK)
    width = LANES * ((blocks - 1) // 2) + depth
    if signal_ref.shape[2] > width:
        begin = pl.multiple_of(lax.axis_index("sub") * t_out, LANES)
    else:
        begin = 0
    own = slice(start, start + count)
    contract = (((1,), (1,)), ((), ()))

    def windows(value):
        odd = pltpu.roll(value, width - BLOCK, 1)
        pieces = []
        for a in range(blocks):
            base = LANES * (a // 2)
            pieces.append((odd if a % 2 else value)[:, base : base + depth])
        return jnp.concatenate(pieces, axis=0)

    waves, squares = [], []
    for channel in range(CHANNELS):
        wave = signal_ref[channel, :, pl.ds(begin, width)].astype(f32)
        half = 0.5 * wave * wave
        upper = half.astype(bf16).astype(f32)
        waves.append(windows(wave).astype(bf16))
        squares += [windows(upper), windows(half - upper)]
    energies = lax.dot_general(
        jnp.concatenate(squares, axis=0).astype(bf16), band_ref[...], contract,
        preferred_element_type=f32,
    ).reshape(2 * CHANNELS, blocks, count, columns)
    coherent = jnp.zeros((blocks, count, columns), f32)
    floor = rows_ref[CHANNELS : CHANNELS + 1, :]
    for channel in range(CHANNELS):
        corr = lax.dot_general(
            waves[channel], toeplitz_ref[channel], contract, preferred_element_type=f32
        ).reshape(blocks, count, columns)
        power = energies[2 * channel] + energies[2 * channel + 1] + floor
        coherent = coherent + corr * weight_ref[channel, own, :] * lax.rsqrt(power)

    tiles = t_out // LANES
    sub = lax.broadcasted_iota(jnp.int32, (8, LANES), 0)
    member = member_ref[own, :].reshape(count // 8, 8, LANES)
    straight = member == (sub >= 4).astype(f32)
    crossed = member == (sub < 4).astype(f32)
    halves = []
    for k in range(share):
        base = LANES * (k // 2)
        target = shift_ref[k, own, :]
        lane = target % BLOCK + BLOCK * (k % 2)
        moved = [
            jnp.take_along_axis(
                coherent[a, :, base : base + LANES], lane, axis=1, mode="promise_in_bounds"
            )
            for a in range(blocks)
        ]
        for tile in range(tiles):
            aligned = jnp.where(
                target < BLOCK,
                moved[2 * tile],
                jnp.where(target < LANES, moved[2 * tile + 1], moved[2 * tile + 2]),
            ).reshape(count // 8, 8, LANES)
            kept = jnp.sum(jnp.where(straight, aligned, 0.0), axis=0)
            other = jnp.sum(jnp.where(crossed, aligned, 0.0), axis=0)
            halves.append(kept + pltpu.roll(other, 4, 0))
    for k in range(0, share, 2):
        for tile in range(tiles):
            first, second = halves[k * tiles + tile], halves[min(k + 1, share - 1) * tiles + tile]
            pair = jnp.where(
                sub % 4 < 2, first + pltpu.roll(first, 6, 0), second + pltpu.roll(second, 2, 0)
            )
            pair = pair + pltpu.roll(pair, 7, 0)
            lanes = slice(tile * LANES, (tile + 1) * LANES)
            for side in range(min(2, share - k)):
                for region in range(REGIONS):
                    at = 4 * region + 2 * side
                    total = pair[at : at + 1, :]
                    if len(partial_and_out) > 1:
                        total = total + partial_and_out[0][k + side, region : region + 1, lanes]
                    out_ref[k + side, region : region + 1, lanes] = total


def shards(traces, trace_tail, templates, win_lengths, moveouts, chan_mask, subnet):
    st_dev, channels, t_dev = traces.shape
    stations = chan_mask.shape[0]
    tmpl_dev, _, span = templates.shape
    t_corr = t_dev + trace_tail.shape[2] - span + 1
    tmpl_count, sta_count = lax.axis_size("tmpl"), lax.axis_size("sta")
    share = tmpl_dev // sta_count
    depth = ceil_to(BLOCK - 1 + span, LANES)
    columns = ceil_to(share * BLOCK, LANES)
    width = LANES * ((-(-t_corr // BLOCK) - 1) // 2) + depth
    vmem = pl.BlockSpec(memory_space=pltpu.VMEM)
    near = lambda value: pltpu.with_memory_space_constraint(value, pltpu.VMEM)

    rounds = []
    for axis, scale in (("tmpl", sta_count), ("sta", 1)):
        bit = lax.axis_size(axis) // 2
        while bit:
            rounds.append((axis, bit, bit * scale))
            bit //= 2
    masks = tuple(mask for _, _, mask in rounds)
    prepared = pl.pallas_call(
        functools.partial(prep_kernel, masks, st_dev, share),
        out_shape=(
            pltpu.VMEM((channels, columns, depth), jnp.bfloat16),
            pltpu.VMEM((columns, depth), jnp.bfloat16),
            pltpu.VMEM((8, columns), jnp.float32),
            pltpu.VMEM((channels, stations, columns), jnp.float32),
            pltpu.VMEM((share, stations, LANES), jnp.int32),
            pltpu.VMEM((stations, LANES), jnp.float32),
        ),
        in_specs=[pl.BlockSpec(memory_space=pltpu.SMEM)] + [vmem] * 4,
        out_specs=(vmem,) * 6,
        scratch_shapes=[pltpu.VMEM((channels, tmpl_dev, depth), jnp.float32)],
        name="prep",
    )(
        win_lengths, jnp.transpose(templates, (1, 0, 2)), jnp.transpose(moveouts),
        jnp.transpose(chan_mask), subnet.reshape(1, -1),
    )
    prepared = tuple(near(value) for value in prepared)

    def stack(start, signal, *partial):
        shape = (share, REGIONS, t_dev)
        operands = (near(signal),) + prepared + partial
        return pl.pallas_call(
            functools.partial(stack_kernel, start, t_corr, t_dev, share),
            out_shape=jax.ShapeDtypeStruct(shape, jnp.float32)
            if partial
            else pltpu.VMEM(shape, jnp.float32),
            in_specs=[vmem] * len(operands),
            out_specs=vmem,
            name="late" if partial else "early",
        )(*operands)

    gathered = whole_rows(traces, trace_tail, t_dev + width)
    for axis, bit, _ in rounds[:-1]:
        gathered = jnp.concatenate([gathered, cross(gathered, axis, bit)], axis=1)
    gathered, member = lax.optimization_barrier((gathered, prepared[-1]))
    prepared = prepared[:-1] + (near(member),)
    wanted = jnp.where(
        lax.axis_index("sub") == 1, gathered[:, :, :width], gathered[:, :, t_dev : t_dev + width]
    )
    arriving = cross(wanted, rounds[-1][0], rounds[-1][1])
    partial = stack(0, gathered)
    return stack(gathered.shape[1], arriving, near(partial))


def solution(mesh):
    in_specs = (
        P(("tmpl", "sta"), None, ("parts", "sub")),
        P(("tmpl", "sta"), None, "parts"),
        P("tmpl", None, None),
        P(),
        P(),
        P("parts", None),
        P(),
    )
    out_specs = P(("tmpl", "sta"), None, ("parts", "sub"))
    return jax.shard_map(shards, mesh=mesh, in_specs=in_specs, out_specs=out_specs, check_vma=False)
```
